32 devices in a mesh: rel: 4 (over y, x), node: 4 (over z), feat: 2 (over core).
Axes of the slice: x: 2, y: 2, z: 4, core: 2. Of those that a mesh axis runs over, the one named last changes fastest.
Arguments:
- features: float32 [3072, 768], P('node', 'feat'), may hold values from -6 to 6
- tile_values: float32 [4, 12, 12, 256, 256], P('rel', 'node'), may hold values from -0.4375 to 0.4375
- tile_cols: int32 [4, 12, 12], P('rel', 'node'), may hold values from 0 to 11, as said below
- tile_count: int32 [4, 12], P('rel', 'node'), may hold values from 1 to 12, as said below
- degree: int32 [4, 3072], P('rel', 'node'), may hold values from 1 to 16
- proj_weight: float32 [4, 768, 512], P('rel', 'feat'), may hold values from -0.21875 to 0.21875
- proj_bias: float32 [4, 512], P('rel', 'feat'), may hold values from -3 to 3
Outputs:
- metapath_out: float32 [4, 3072, 512], P(None, ('node', 'rel'), 'feat')
The draws below stay inside these ranges and needn't reach their ends.
Inputs may be any that keep to these rules, and one draw needn't show every extreme that they name: `tile_cols`: within one row of tiles the 12 column tiles are distinct; slots at or past the count hold valid tile numbers that are not used. `tile_count`: in every relation some row of tiles has exactly 12 live slots.
All inputs are finite; a program needn't handle non-finite values.
Results may differ from the reference program's by a relative error of at most 0.0001.
Values sent between devices are 32-bit elements; how exact they have to be, the bound alone decides.
A program may use at most 128 MiB of HBM per device.

```python
import jax
import jax.numpy as jnp
from jax import lax

F = 768
HID = 512
TILE = 256
K = 12
REL = 4
NODES = 3072
NTILES = 12


def draw_tile_cols(key, part):
    row_keys = jax.random.split(key, REL * NTILES)

    def choose(one_key):
        return jax.random.permutation(one_key, NTILES)[:K]
    picked = jax.vmap(choose)(row_keys)
    return picked.reshape(REL, NTILES, K).astype(jnp.int32)


def draw_tile_count(key, part):
    drawn = jax.random.randint(key, (REL, NTILES), 1, K + 1)
    full_row = jax.random.randint(jax.random.fold_in(key, 7), (REL,), 0, NTILES)
    is_full = jnp.arange(NTILES)[None, :] == full_row[:, None]
    return jnp.where(is_full, K, drawn).astype(jnp.int32)


def place_ends(array, stream_key, smallest, high):
    longest = array.shape.index(max(array.shape))
    spots = []
    for shift in (0, 1):
        where = [jax.random.randint(jax.random.fold_in(stream_key, axis), (), 0, length) for axis, length in enumerate(array.shape)]
        where[longest] = (where[longest] + shift) % array.shape[longest]
        spots.append(tuple(where))
    return array.at[spots[0]].set(smallest).at[spots[1]].set(high)


def block_levels(own_key, dims, cuts, smallest, top_value):
    def one(axis_at, shards_of):
        draws = jax.random.uniform(jax.random.fold_in(jax.random.fold_in(own_key, 6), axis_at), (shards_of,), jnp.float32, smallest / len(cuts), top_value / len(cuts))
        return jnp.repeat(jnp.exp(draws), dims[axis_at] // shards_of).reshape((-1,) + (1,) * (len(dims) - axis_at - 1))

    level = one(*cuts[0])
    for cut in cuts[1:]:
        level = level * one(*cut)
    return level


def noise(stream_key, shape, width, bound, shards=(), held_as=jnp.bfloat16):
    factor_of = block_levels(stream_key, shape, shards, -0.22, 0.18) if shards else 1.0
    values = jax.random.normal(stream_key, shape, jnp.float32) * width * factor_of
    return jnp.minimum(jnp.maximum(values, -bound), bound).astype(held_as)


def setup_inputs(seed: int = 0) -> dict:
    arg_keys = jax.random.split(jax.random.key(seed), 8)
    return {
        "features": noise(arg_keys[0], (NODES, F), 1.0, 6.0, ((0, 4), (1, 2)), jnp.float32),
        "tile_values": noise(arg_keys[1], (REL, NTILES, K, TILE, TILE), (TILE * K // 16) ** -0.5, 0.4375, ((0, 4), (1, 4)), jnp.float32),
        "tile_cols": draw_tile_cols(jax.random.fold_in(arg_keys[7], 71), 0),
        "tile_count": draw_tile_count(jax.random.fold_in(arg_keys[7], 71), 0),
        "degree": place_ends(jax.random.randint(arg_keys[4], (REL, NODES), 1, 17), jax.random.fold_in(arg_keys[4], 1), 1, 16).astype(jnp.int32),
        "proj_weight": noise(arg_keys[5], (REL, F, HID), F ** -0.5, 0.21875, ((0, 4), (1, 2)), jnp.float32),
        "proj_bias": noise(arg_keys[6], (REL, HID), 0.5, 3.0, ((0, 4), (1, 2)), jnp.float32),
    }


def one_hop(current, values, cols, count, row_scale):
    columns = current.shape[1]
    tile_rows = (row_scale[:, None] * current).reshape(NTILES, TILE, columns)
    live_mask = (jnp.arange(K)[None, :] < count[:, None]).astype(current.dtype)

    def row_tile(items):
        values_row, cols_row, mask_row = items
        sources = tile_rows[cols_row]
        kept = values_row * mask_row[:, None, None]
        return jnp.einsum('kab,kbw->aw', kept, sources, precision=lax.Precision.HIGHEST)
    summed = lax.map(row_tile, (values, cols, live_mask))
    return row_scale[:, None] * summed.reshape(NODES, columns)

def reference(features, tile_values, tile_cols, tile_count, degree, proj_weight, proj_bias):
    results = []
    for relation in range(REL):
        row_scale = lax.rsqrt(degree[relation].astype(jnp.float32))
        first = one_hop(features, tile_values[relation], tile_cols[relation], tile_count[relation], row_scale)
        second = one_hop(first, tile_values[relation], tile_cols[relation], tile_count[relation], row_scale)
        projected = jnp.dot(second, proj_weight[relation], precision=lax.Precision.HIGHEST, preferred_element_type=jnp.float32)
        results.append(projected + proj_bias[relation][None, :])
    return jnp.stack(results)
```

```python
import jax
import jax.numpy as jnp
from jax import lax
from jax.sharding import PartitionSpec as P


def spread(gathered, masked, col_tiles):
    columns = gathered.shape[1]
    tile_rows = gathered.reshape(-1, masked.shape[2], columns)
    sources = jnp.take(tile_rows, col_tiles, axis=0)
    summed = jnp.einsum(
        "tkab,tkbw->taw",
        masked,
        sources,
        precision=lax.Precision.HIGH,
        preferred_element_type=jnp.float32,
    )
    return summed.reshape(-1, columns)


def on_device(features, tile_values, tile_cols, tile_count, degree, proj_weight, proj_bias):
    row_scale = lax.rsqrt(degree[0].astype(jnp.float32))[:, None]
    counts = tile_count[0]
    live_mask = (jnp.arange(tile_values.shape[2])[None, :] < counts[:, None]).astype(jnp.float32)
    masked = tile_values[0] * live_mask[:, :, None, None]
    col_tiles = tile_cols[0]
    partial_sum = jnp.dot(
        features, proj_weight[0], precision=lax.Precision.HIGH, preferred_element_type=jnp.float32
    )
    current = lax.psum_scatter(partial_sum, "feat", scatter_dimension=1, tiled=True)
    for hop_index in range(2):
        gathered = lax.all_gather(row_scale * current, "node", axis=0, tiled=True)
        current = row_scale * spread(gathered, masked, col_tiles)
    result = current + proj_bias[0][None, :]
    return lax.all_to_all(result[None], "rel", split_axis=1, concat_axis=0, tiled=True)


def solution(mesh):
    return jax.shard_map(
        on_device,
        mesh=mesh,
        in_specs=(
            P("node", "feat"),
            P("rel", "node", None, None, None),
            P("rel", "node", None),
            P("rel", "node"),
            P("rel", "node"),
            P("rel", "feat", None),
            P("rel", "feat"),
        ),
        out_specs=P(None, ("node", "rel"), "feat"),
        check_vma=False,
    )
```

```python
import functools

import jax
import jax.numpy as jnp
from jax import lax
from jax.experimental import pallas as pl
from jax.experimental.pallas import tpu as pltpu
from jax.sharding import PartitionSpec as P

MESH = pl.DeviceIdType.MESH
LANES = 128
HOPS = 2


def split(x):
    high = x.astype(jnp.bfloat16)
    return high, (x - high.astype(jnp.float32)).astype(jnp.bfloat16)


def paired(x):
    high, low = split(x)
    return high, jnp.concatenate([high, low], axis=1)


def product(a, x_high, x_pair):
    a_high, a_low = split(a)
    both = jnp.dot(a_high, x_pair, preferred_element_type=jnp.float32)
    rest = jnp.dot(a_low, x_high, preferred_element_type=jnp.float32)
    return both[:, :LANES] + both[:, LANES:] + rest


def kernel(
    sizes,
    slot_of,
    live,
    features,
    weight,
    scale,
    bias,
    tiles_hbm,
    out,
    tiles,
    field,
    total,
    result,
    partial_out,
    partial_in,
    tiles_sem,
    pair_send,
    pair_recv,
    line_send,
    line_recv,
    out_send,
    out_recv,
):
    nodes, rels, chunks = sizes
    rows = features.shape[0]
    tile = tiles.shape[2]
    row_tiles = tiles.shape[0]
    col_tiles = nodes * row_tiles
    group = rows // rels
    rel, node, feat = (lax.axis_index(name) for name in ("rel", "node", "feat"))
    has_up, has_down = node < nodes - 1, node > 0

    tiles_copy = pltpu.make_async_copy(tiles_hbm, tiles, tiles_sem)
    tiles_copy.start()

    barrier = pltpu.get_barrier_semaphore()
    pl.semaphore_signal(barrier, inc=1, device_id={"feat": 1 - feat}, device_id_type=MESH)
    for step in range(1, rels):
        peer = lax.rem(rel + step, rels)
        pl.semaphore_signal(barrier, inc=1, device_id={"rel": peer}, device_id_type=MESH)

    @pl.when(has_up)
    def _():
        pl.semaphore_signal(barrier, inc=1, device_id={"node": node + 1}, device_id_type=MESH)

    @pl.when(has_down)
    def _():
        pl.semaphore_signal(barrier, inc=1, device_id={"node": node - 1}, device_id_type=MESH)

    peers = rels + has_up.astype(jnp.int32) + has_down.astype(jnp.int32)
    pl.semaphore_wait(barrier, peers)

    def line_copy(stage, way, slot):
        neighbour = node + 1 if way == 0 else node - 1
        return pltpu.make_async_remote_copy(
            src_ref=field.at[stage, slot],
            dst_ref=field.at[stage, slot],
            send_sem=line_send.at[stage, way, slot],
            recv_sem=line_recv.at[stage, slot],
            device_id={"node": neighbour},
            device_id_type=MESH,
        )

    def send_up(stage, slot):
        @pl.when(has_up)
        def _():
            line_copy(stage, 0, slot).start()

    def send_down(stage, slot):
        @pl.when(has_down)
        def _():
            line_copy(stage, 1, slot).start()

    def accumulate(stage, slot):
        def one_tile(j, carry):
            x = field[stage, slot, pl.ds(pl.multiple_of(j * tile, tile), tile), :]
            x_high, x_pair = paired(x)
            for t in range(row_tiles):
                place = t * col_tiles + slot * row_tiles + j
                a = tiles[t, slot_of[place]] * live[place]
                total[t * tile : (t + 1) * tile, :] += product(a, x_high, x_pair)
            return carry

        lax.fori_loop(0, row_tiles, one_tile, 0)

    def hop(stage):
        total[...] = jnp.zeros_like(total)
        accumulate(stage, node)

        def step(s, carry):
            @pl.when(node - s >= 0)
            def _():
                line_copy(stage, 0, node - s).wait_recv()
                send_up(stage, node - s)

            @pl.when(node + s < nodes)
            def _():
                line_copy(stage, 1, node + s).wait_recv()
                send_down(stage, node + s)

            @pl.when(node - s >= 0)
            def _():
                accumulate(stage, node - s)

            @pl.when(node + s < nodes)
            def _():
                accumulate(stage, node + s)

            return carry

        lax.fori_loop(1, nodes, step, 0)

    def begin(stage):
        send_up(stage, node)
        send_down(stage, node)

    def project(side, chunk, target):
        start = pl.multiple_of((side * chunks + chunk) * LANES, LANES)
        w_high, w_pair = paired(weight[:, pl.ds(start, LANES)])

        def some_rows(j, carry):
            place = pl.ds(pl.multiple_of(j * tile, tile), tile)
            target(place, product(features[place, :], w_high, w_pair))
            return carry

        lax.fori_loop(0, row_tiles, some_rows, 0)

    def pair_copy(chunk):
        return pltpu.make_async_remote_copy(
            src_ref=partial_out.at[chunk],
            dst_ref=partial_in.at[chunk],
            send_sem=pair_send.at[chunk],
            recv_sem=pair_recv.at[chunk],
            device_id={"feat": 1 - feat},
            device_id_type=MESH,
        )

    for chunk in range(chunks):

        def keep_out(place, value, chunk=chunk):
            partial_out[chunk, place, :] = value

        project(1 - feat, chunk, keep_out)
        pair_copy(chunk).start()
    for chunk in range(chunks):

        def keep_own(place, value, chunk=chunk):
            field[chunk, node, place, :] = value

        project(feat, chunk, keep_own)
        pair_copy(chunk).wait_recv()
        field[chunk, node] = scale[...] * (field[chunk, node] + partial_in[chunk])
        begin(chunk)

    tiles_copy.wait()

    for chunk in range(chunks):
        hop(chunk)
        field[chunks + chunk, node] = scale[...] * (scale[...] * total[...])
        begin(chunks + chunk)

    def out_copy(chunk, step):
        peer = lax.rem(rel + step, rels)
        return pltpu.make_async_remote_copy(
            src_ref=result.at[chunk, pl.ds(pl.multiple_of(peer * group, 8), group), :],
            dst_ref=out.at[rel, :, pl.ds(chunk * LANES, LANES)],
            send_sem=out_send.at[chunk, step],
            recv_sem=out_recv.at[chunk, step],
            device_id={"rel": peer},
            device_id_type=MESH,
        )

    def in_copy(chunk, step):
        peer = lax.rem(rel + rels - step, rels)
        return pltpu.make_async_remote_copy(
            src_ref=result.at[chunk, pl.ds(0, group), :],
            dst_ref=out.at[peer, :, pl.ds(chunk * LANES, LANES)],
            send_sem=out_send.at[chunk, step],
            recv_sem=out_recv.at[chunk, step],
            device_id={"rel": peer},
            device_id_type=MESH,
        )

    for chunk in range(chunks):
        hop(chunks + chunk)
        columns = slice(chunk * LANES, (chunk + 1) * LANES)
        result[chunk] = scale[...] * total[...] + bias[:, columns]
        for step in range(1, rels):
            out_copy(chunk, step).start()
        own = pl.ds(pl.multiple_of(rel * group, 8), group)
        out[rel, :, columns] = result[chunk, own, :]

    for chunk in range(chunks):
        pair_copy(chunk).wait_send()
        for step in range(1, rels):
            out_copy(chunk, step).wait_send()
            in_copy(chunk, step).wait_recv()
    for stage in range(HOPS * chunks):

        def drain(slot, carry, stage=stage):
            @pl.when(jnp.logical_and(has_up, slot <= node))
            def _():
                line_copy(stage, 0, slot).wait_send()

            @pl.when(jnp.logical_and(has_down, slot >= node))
            def _():
                line_copy(stage, 1, slot).wait_send()

            return carry

        lax.fori_loop(0, nodes, drain, 0)


def on_device(
    nodes, rels, features, tile_values, tile_cols, tile_count, degree, proj_weight, proj_bias
):
    rows, depth = features.shape
    _, row_tiles, slots, tile, _ = tile_values.shape
    width = proj_bias.shape[1]
    chunks = width // LANES
    col_tiles = nodes * row_tiles
    stages = HOPS * chunks
    scale = jnp.broadcast_to(lax.rsqrt(degree[0].astype(jnp.float32))[:, None], (rows, LANES))
    places = jnp.arange(slots)
    used = places[None, :] < tile_count[0][:, None]
    hit = (tile_cols[0][:, None, :] == jnp.arange(col_tiles)[None, :, None]) & used[:, None, :]
    slot_of = jnp.sum(jnp.where(hit, places[None, None, :], 0), axis=2).astype(jnp.int32)
    live = jnp.sum(hit.astype(jnp.float32), axis=2)
    vmem = pl.BlockSpec(memory_space=pltpu.VMEM)
    smem = pl.BlockSpec(memory_space=pltpu.SMEM)
    dma = pltpu.SemaphoreType.DMA
    return pl.pallas_call(
        functools.partial(kernel, (nodes, rels, chunks)),
        out_shape=jax.ShapeDtypeStruct((rels, rows // rels, width), jnp.float32),
        in_specs=[smem, smem, vmem, vmem, vmem, vmem, pl.BlockSpec(memory_space=pl.ANY)],
        out_specs=vmem,
        scratch_shapes=[
            pltpu.VMEM((row_tiles, slots, tile, tile), jnp.float32),
            pltpu.VMEM((stages, nodes, rows, LANES), jnp.float32),
            pltpu.VMEM((rows, LANES), jnp.float32),
            pltpu.VMEM((chunks, rows, LANES), jnp.float32),
            pltpu.VMEM((chunks, rows, LANES), jnp.float32),
            pltpu.VMEM((chunks, rows, LANES), jnp.float32),
            dma,
            dma((chunks,)),
            dma((chunks,)),
            dma((stages, 2, nodes)),
            dma((stages, nodes)),
            dma((chunks, rels)),
            dma((chunks, rels)),
        ],
        compiler_params=pltpu.CompilerParams(
            collective_id=0, has_side_effects=True, vmem_limit_bytes=56 << 20
        ),
    )(
        slot_of.reshape(-1),
        live.reshape(-1),
        features,
        proj_weight[0],
        scale,
        proj_bias,
        tile_values[0],
    )


def solution(mesh):
    return jax.shard_map(
        functools.partial(on_device, mesh.shape["node"], mesh.shape["rel"]),
        mesh=mesh,
        in_specs=(
            P("node", "feat"),
            P("rel", "node", None, None, None),
            P("rel", "node", None),
            P("rel", "node"),
            P("rel", "node"),
            P("rel", "feat", None),
            P("rel", "feat"),
        ),
        out_specs=P(None, ("node", "rel"), "feat"),
        check_vma=False,
    )
```

```python
import functools

import jax
import jax.numpy as jnp
from jax import lax
from jax.experimental import pallas as pl
from jax.experimental.pallas import tpu as pltpu
from jax.sharding import PartitionSpec as P

MESH = pl.DeviceIdType.MESH
LANES = 128
SUBLANES = 8


def split(x):
    high = x.astype(jnp.bfloat16)
    return high, (x - high.astype(jnp.float32)).astype(jnp.bfloat16)


def paired(x):
    high, low = split(x)
    return high, jnp.concatenate([high, low], axis=1)


def product(a, x_high, x_pair):
    a_high, a_low = split(a)
    width = x_high.shape[1]
    both = jnp.dot(a_high, x_pair, preferred_element_type=jnp.float32)
    rest = jnp.dot(a_low, x_high, preferred_element_type=jnp.float32)
    return both[:, :width] + both[:, width:] + rest


def kernel(
    sizes,
    slot_of,
    live,
    source_scale,
    weight,
    scale,
    bias,
    features_hbm,
    tiles_hbm,
    out,
    tiles,
    raw,
    scales,
    first,
    field,
    total,
    result,
    partial_out,
    partial_in,
    load_sem,
    scale_send,
    scale_recv,
    z_send,
    z_recv,
    x_send,
    x_recv,
    y_send,
    y_recv,
    pair_send,
    pair_recv,
    line_send,
    line_recv,
    out_send,
    out_recv,
):
    nodes, rels, chunks = sizes
    rows, depth = raw.shape[1:]
    tile = tiles.shape[2]
    row_tiles = tiles.shape[0]
    col_tiles = nodes * row_tiles
    group = rows // rels
    parts = depth // LANES
    rel, node, feat = (lax.axis_index(name) for name in ("rel", "node", "feat"))
    has_up, has_down = node < nodes - 1, node > 0
    x_rel, y_rel, far_rel = rel + 1 - 2 * lax.rem(rel, 2), lax.rem(rel + 2, rels), rels - 1 - rel

    barrier = pltpu.get_barrier_semaphore()
    pl.semaphore_signal(barrier, inc=1, device_id={"feat": 1 - feat}, device_id_type=MESH)
    for step in range(1, rels):
        peer = lax.rem(rel + step, rels)
        pl.semaphore_signal(barrier, inc=1, device_id={"rel": peer}, device_id_type=MESH)
    for step in range(1, nodes):
        peer = lax.rem(node + step, nodes)
        pl.semaphore_signal(barrier, inc=1, device_id={"node": peer}, device_id_type=MESH)
    features_copy = pltpu.make_async_copy(features_hbm, raw.at[node], load_sem.at[0])
    features_copy.start()
    tiles_copy = pltpu.make_async_copy(tiles_hbm, tiles, load_sem.at[1])
    tiles_copy.start()
    scales[node] = source_scale[...]
    features_copy.wait()
    pl.semaphore_wait(barrier, rels + nodes - 1)

    def remote(src, dst, send_sem, recv_sem, **device):
        return pltpu.make_async_remote_copy(
            src_ref=src,
            dst_ref=dst,
            send_sem=send_sem,
            recv_sem=recv_sem,
            device_id=device,
            device_id_type=MESH,
        )

    def scale_copy(slot, step):
        peer = lax.rem(node + step, nodes)
        return remote(
            scales.at[slot], scales.at[slot], scale_send.at[step], scale_recv.at[slot], node=peer
        )

    def piece(slot, quarter, part):
        place = pl.ds(pl.multiple_of(quarter * group, 8), group)
        return raw.at[slot, place, pl.ds(part * LANES, LANES)]

    def z_copy(way, slot, p):
        ref = piece(slot, rel, p) if p < parts else piece(slot, far_rel, 0)
        neighbour = node + 1 if way == 0 else node - 1
        return remote(ref, ref, z_send.at[way, slot, p], z_recv.at[slot, p], node=neighbour)

    def x_copy(slot, p, near, far):
        ref = piece(slot, near, p) if p < parts else piece(slot, far, 1)
        return remote(ref, ref, x_send.at[slot, p], x_recv.at[slot, p], rel=x_rel)

    def y_copy(slot, p, near, far):
        ref = piece(slot, near, p) if p < parts else piece(slot, far, 2)
        return remote(ref, ref, y_send.at[slot, p], y_recv.at[slot, p], rel=y_rel)

    def x_out(slot, p):
        return x_copy(slot, p, rel, y_rel)

    def x_in(slot, p):
        return x_copy(slot, p, x_rel, far_rel)

    def y_out(slot, p):
        return y_copy(slot, p, rel, x_rel)

    def y_in(slot, p):
        return y_copy(slot, p, y_rel, far_rel)

    def take_z(way, slot):
        onward = has_up if way == 0 else has_down
        for p in range(parts + 1):
            z_copy(way, slot, p).wait_recv()

            @pl.when(onward)
            def _(p=p):
                z_copy(way, slot, p).start()

            if p < parts:
                x_out(slot, p).start()
                y_out(slot, p).start()

    def take_xy(slot):
        for p in range(parts):
            x_in(slot, p).wait_recv()
            if p == 2:
                y_out(slot, parts).start()
            y_in(slot, p).wait_recv()
            if p == 1:
                x_out(slot, parts).start()
        x_in(slot, parts).wait_recv()
        y_in(slot, parts).wait_recv()

    def both_sides(s, act):
        @pl.when(node - s >= 0)
        def _():
            act(0, node - s)

        @pl.when(node + s < nodes)
        def _():
            act(1, node + s)

    for step in range(1, nodes):
        scale_copy(node, step).start()
    for p in range(parts + 1):

        @pl.when(has_up)
        def _(p=p):
            z_copy(0, node, p).start()

        @pl.when(has_down)
        def _(p=p):
            z_copy(1, node, p).start()

    def accumulate_first(slot):
        def one_tile(j, carry):
            x = raw[slot, pl.ds(pl.multiple_of(j * tile, tile), tile), :]
            x_high, x_pair = paired(x)
            column_scale = scales[slot, pl.ds(j, 1), :]
            for t in range(row_tiles):
                place = t * col_tiles + slot * row_tiles + j
                a = tiles[t, slot_of[place]] * (column_scale * live[place])
                first[t * tile : (t + 1) * tile, :] += product(a, x_high, x_pair)
            return carry

        lax.fori_loop(0, row_tiles, one_tile, 0)

    both_sides(1, take_z)
    first[...] = jnp.zeros_like(first)
    tiles_copy.wait()
    accumulate_first(node)

    def first_step(s, carry):
        both_sides(s + 1, take_z)
        both_sides(s, lambda way, slot: take_xy(slot))

        def use(way, slot):
            scale_copy(slot, 1).wait_recv()
            accumulate_first(slot)

        both_sides(s, use)
        return carry

    lax.fori_loop(1, nodes, first_step, 0)

    def line_copy(stage, way, slot):
        neighbour = node + 1 if way == 0 else node - 1
        ref = field.at[stage, slot]
        return remote(
            ref, ref, line_send.at[stage, way, slot], line_recv.at[stage, slot], node=neighbour
        )

    def send_up(stage, slot):
        @pl.when(has_up)
        def _():
            line_copy(stage, 0, slot).start()

    def send_down(stage, slot):
        @pl.when(has_down)
        def _():
            line_copy(stage, 1, slot).start()

    def accumulate(stage, slot):
        def one_tile(j, carry):
            x = field[stage, slot, pl.ds(pl.multiple_of(j * tile, tile), tile), :]
            x_high, x_pair = paired(x)
            for t in range(row_tiles):
                place = t * col_tiles + slot * row_tiles + j
                a = tiles[t, slot_of[place]] * live[place]
                total[t * tile : (t + 1) * tile, :] += product(a, x_high, x_pair)
            return carry

        lax.fori_loop(0, row_tiles, one_tile, 0)

    def hop(stage):
        total[...] = jnp.zeros_like(total)
        accumulate(stage, node)

        def step(s, carry):
            @pl.when(node - s >= 0)
            def _():
                line_copy(stage, 0, node - s).wait_recv()
                send_up(stage, node - s)

            @pl.when(node + s < nodes)
            def _():
                line_copy(stage, 1, node + s).wait_recv()
                send_down(stage, node + s)

            both_sides(s, lambda way, slot: accumulate(stage, slot))
            return carry

        lax.fori_loop(1, nodes, step, 0)

    def project(side, chunk, target):
        start = pl.multiple_of((side * chunks + chunk) * LANES, LANES)
        w_high, w_pair = paired(weight[:, pl.ds(start, LANES)])

        def some_rows(j, carry):
            place = pl.ds(pl.multiple_of(j * tile, tile), tile)
            target[place, :] = product(first[place, :], w_high, w_pair)
            return carry

        lax.fori_loop(0, row_tiles, some_rows, 0)

    def pair_copy(chunk):
        return remote(
            partial_out.at[chunk],
            partial_in.at[chunk],
            pair_send.at[chunk],
            pair_recv.at[chunk],
            feat=1 - feat,
        )

    def give(chunk):
        project(1 - feat, chunk, partial_out.at[chunk])
        pair_copy(chunk).start()

    give(0)
    for chunk in range(chunks):
        project(feat, chunk, field.at[chunk, node])
        if chunk + 1 < chunks:
            give(chunk + 1)
        pair_copy(chunk).wait_recv()
        field[chunk, node] = scale[...] * (
            scale[...] * (field[chunk, node] + partial_in[chunk])
        )
        send_up(chunk, node)
        send_down(chunk, node)

    def out_copy(chunk, step):
        peer = lax.rem(rel + step, rels)
        return remote(
            result.at[chunk, pl.ds(pl.multiple_of(peer * group, 8), group), :],
            out.at[rel, :, pl.ds(chunk * LANES, LANES)],
            out_send.at[chunk, step],
            out_recv.at[chunk, step],
            rel=peer,
        )

    def in_copy(chunk, step):
        peer = lax.rem(rel + rels - step, rels)
        return remote(
            result.at[chunk, pl.ds(0, group), :],
            out.at[peer, :, pl.ds(chunk * LANES, LANES)],
            out_send.at[chunk, step],
            out_recv.at[chunk, step],
            rel=peer,
        )

    for chunk in range(chunks):
        hop(chunk)
        columns = slice(chunk * LANES, (chunk + 1) * LANES)
        result[chunk] = scale[...] * total[...] + bias[:, columns]
        for step in range(1, rels):
            out_copy(chunk, step).start()
        own = pl.ds(pl.multiple_of(rel * group, 8), group)
        out[rel, :, columns] = result[chunk, own, :]

    for step in range(1, nodes):
        scale_copy(node, step).wait_send()

    def drain(slot, carry):
        def waits(way):
            for p in range(parts + 1):
                z_copy(way, slot, p).wait_send()
            for stage in range(chunks):
                line_copy(stage, way, slot).wait_send()

        @pl.when(jnp.logical_and(has_up, slot <= node))
        def _():
            waits(0)

        @pl.when(jnp.logical_and(has_down, slot >= node))
        def _():
            waits(1)

        @pl.when(slot != node)
        def _():
            for p in range(parts + 1):
                x_out(slot, p).wait_send()
                y_out(slot, p).wait_send()

        return carry

    lax.fori_loop(0, nodes, drain, 0)
    for chunk in range(chunks):
        pair_copy(chunk).wait_send()
        for step in range(1, rels):
            out_copy(chunk, step).wait_send()
            in_copy(chunk, step).wait_recv()


def on_device(
    nodes, rels, features, tile_values, tile_cols, tile_count, degree, proj_weight, proj_bias
):
    rows, depth = features.shape
    _, row_tiles, slots, tile, _ = tile_values.shape
    width = proj_bias.shape[1]
    chunks = width // LANES
    col_tiles = nodes * row_tiles
    parts = depth // LANES + 1
    row_scale = lax.rsqrt(degree[0].astype(jnp.float32))
    scale = jnp.broadcast_to(row_scale[:, None], (rows, LANES))
    source_scale = jnp.pad(row_scale.reshape(row_tiles, tile), ((0, SUBLANES - row_tiles), (0, 0)))
    places = jnp.arange(slots)
    used = places[None, :] < tile_count[0][:, None]
    hit = (tile_cols[0][:, None, :] == jnp.arange(col_tiles)[None, :, None]) & used[:, None, :]
    slot_of = jnp.sum(jnp.where(hit, places[None, None, :], 0), axis=2).astype(jnp.int32)
    live = jnp.sum(hit.astype(jnp.float32), axis=2)
    vmem = pl.BlockSpec(memory_space=pltpu.VMEM)
    smem = pl.BlockSpec(memory_space=pltpu.SMEM)
    dma = pltpu.SemaphoreType.DMA
    return pl.pallas_call(
        functools.partial(kernel, (nodes, rels, chunks)),
        out_shape=jax.ShapeDtypeStruct((rels, rows // rels, width), jnp.float32),
        in_specs=[smem, smem, vmem, vmem, vmem, vmem] + [pl.BlockSpec(memory_space=pl.ANY)] * 2,
        out_specs=vmem,
        scratch_shapes=[
            pltpu.VMEM((row_tiles, slots, tile, tile), jnp.float32),
            pltpu.VMEM((nodes, rows, depth), jnp.float32),
            pltpu.VMEM((nodes, SUBLANES, tile), jnp.float32),
            pltpu.VMEM((rows, depth), jnp.float32),
            pltpu.VMEM((chunks, nodes, rows, LANES), jnp.float32),
            pltpu.VMEM((rows, LANES), jnp.float32),
            pltpu.VMEM((chunks, rows, LANES), jnp.float32),
            pltpu.VMEM((chunks, rows, LANES), jnp.float32),
            pltpu.VMEM((chunks, rows, LANES), jnp.float32),
            dma((2,)),
            dma((nodes,)),
            dma((nodes,)),
            dma((2, nodes, parts)),
            dma((nodes, parts)),
            dma((nodes, parts)),
            dma((nodes, parts)),
            dma((nodes, parts)),
            dma((nodes, parts)),
            dma((chunks,)),
            dma((chunks,)),
            dma((chunks, 2, nodes)),
            dma((chunks, nodes)),
            dma((chunks, rels)),
            dma((chunks, rels)),
        ],
        compiler_params=pltpu.CompilerParams(
            collective_id=0, has_side_effects=True, vmem_limit_bytes=56 << 20
        ),
    )(
        slot_of.reshape(-1),
        live.reshape(-1),
        source_scale,
        proj_weight[0],
        scale,
        proj_bias,
        features,
        tile_values[0],
    )


def solution(mesh):
    return jax.shard_map(
        functools.partial(on_device, mesh.shape["node"], mesh.shape["rel"]),
        mesh=mesh,
        in_specs=(
            P("node", "feat"),
            P("rel", "node", None, None, None),
            P("rel", "node", None),
            P("rel", "node"),
            P("rel", "node"),
            P("rel", "feat", None),
            P("rel", "feat"),
        ),
        out_specs=P(None, ("node", "rel"), "feat"),
        check_vma=False,
    )
```

```python
import functools

import jax
import jax.numpy as jnp
from jax import lax
from jax.experimental import pallas as pl
from jax.experimental.pallas import tpu as pltpu
from jax.sharding import PartitionSpec as P

MESH = pl.DeviceIdType.MESH
LANES = 128
SUBLANES = 8


def split(x):
    high = x.astype(jnp.bfloat16)
    return high, (x - high.astype(jnp.float32)).astype(jnp.bfloat16)


def paired(x):
    high, low = split(x)
    return high, jnp.concatenate([high, low], axis=1)


def product(a, x_high, x_pair):
    a_high, a_low = split(a)
    width = x_high.shape[1]
    both = jnp.dot(a_high, x_pair, preferred_element_type=jnp.float32)
    rest = jnp.dot(a_low, x_high, preferred_element_type=jnp.float32)
    return both[:, :width] + both[:, width:] + rest


def kernel(
    sizes,
    tile_cols,
    tile_count,
    degree,
    weight,
    bias,
    features_hbm,
    tiles_hbm,
    out,
    slot_of,
    live,
    scale,
    tiles,
    raw,
    scales,
    first,
    field,
    total,
    result,
    partial_out,
    partial_in,
    load_sem,
    scale_send,
    scale_recv,
    z_send,
    z_recv,
    x_send,
    x_recv,
    y_send,
    y_recv,
    pair_send,
    pair_recv,
    line_send,
    line_recv,
    out_send,
    out_recv,
):
    nodes, rels, chunks = sizes
    parts, rows = raw.shape[1:3]
    slots = tiles.shape[1]
    tile = tiles.shape[2]
    row_tiles = tiles.shape[0]
    col_tiles = nodes * row_tiles
    group = rows // rels
    rel, node, feat = (lax.axis_index(name) for name in ("rel", "node", "feat"))
    has_up, has_down = node < nodes - 1, node > 0
    x_rel, y_rel, far_rel = rel + 1 - 2 * lax.rem(rel, 2), lax.rem(rel + 2, rels), rels - 1 - rel

    barrier = pltpu.get_barrier_semaphore()
    pl.semaphore_signal(barrier, inc=1, device_id={"feat": 1 - feat}, device_id_type=MESH)
    for step in range(1, rels):
        peer = lax.rem(rel + step, rels)
        pl.semaphore_signal(barrier, inc=1, device_id={"rel": peer}, device_id_type=MESH)
    for step in range(1, nodes):
        peer = lax.rem(node + step, nodes)
        pl.semaphore_signal(barrier, inc=1, device_id={"node": peer}, device_id_type=MESH)
    features_copies = [
        pltpu.make_async_copy(
            features_hbm.at[:, pl.ds(p * LANES, LANES)], raw.at[node, p], load_sem.at[p]
        )
        for p in range(parts)
    ]
    for copy in features_copies:
        copy.start()
    tiles_copy = pltpu.make_async_copy(tiles_hbm, tiles, load_sem.at[parts])
    tiles_copy.start()
    row_scale = lax.rsqrt(degree[...].astype(jnp.float32))
    scales[node] = jnp.zeros(scales.shape[1:], jnp.float32)
    for t in range(row_tiles):
        scales[node, t : t + 1, :] = row_scale[:, t * tile : (t + 1) * tile]
    for copy in features_copies:
        copy.wait()
    pl.semaphore_wait(barrier, rels + nodes - 1)

    def remote(src, dst, send_sem, recv_sem, **device):
        return pltpu.make_async_remote_copy(
            src_ref=src,
            dst_ref=dst,
            send_sem=send_sem,
            recv_sem=recv_sem,
            device_id=device,
            device_id_type=MESH,
        )

    def scale_copy(slot, step):
        peer = lax.rem(node + step, nodes)
        return remote(
            scales.at[slot], scales.at[slot], scale_send.at[step], scale_recv.at[slot], node=peer
        )

    def piece(slot, quarter, part):
        place = pl.ds(pl.multiple_of(quarter * group, 8), group)
        return raw.at[slot, part, place, :]

    def z_copy(way, slot, p):
        ref = piece(slot, rel, p) if p < parts else piece(slot, far_rel, 0)
        neighbour = node + 1 if way == 0 else node - 1
        return remote(ref, ref, z_send.at[way, slot, p], z_recv.at[slot, p], node=neighbour)

    def x_copy(slot, p, near, far):
        ref = piece(slot, near, p) if p < parts else piece(slot, far, 1)
        return remote(ref, ref, x_send.at[slot, p], x_recv.at[slot, p], rel=x_rel)

    def y_copy(slot, p, near, far):
        ref = piece(slot, near, p) if p < parts else piece(slot, far, 2)
        return remote(ref, ref, y_send.at[slot, p], y_recv.at[slot, p], rel=y_rel)

    def x_out(slot, p):
        return x_copy(slot, p, rel, y_rel)

    def x_in(slot, p):
        return x_copy(slot, p, x_rel, far_rel)

    def y_out(slot, p):
        return y_copy(slot, p, rel, x_rel)

    def y_in(slot, p):
        return y_copy(slot, p, y_rel, far_rel)

    def take_z(way, slot):
        onward = has_up if way == 0 else has_down
        for p in range(parts + 1):
            z_copy(way, slot, p).wait_recv()

            @pl.when(onward)
            def _(p=p):
                z_copy(way, slot, p).start()

            if p < parts:
                x_out(slot, p).start()
                y_out(slot, p).start()

    def take_xy(slot):
        for p in range(parts):
            x_in(slot, p).wait_recv()
            if p == 2:
                y_out(slot, parts).start()
            y_in(slot, p).wait_recv()
            if p == 1:
                x_out(slot, parts).start()
        x_in(slot, parts).wait_recv()
        y_in(slot, parts).wait_recv()

    def both_sides(s, act):
        @pl.when(node - s >= 0)
        def _():
            act(0, node - s)

        @pl.when(node + s < nodes)
        def _():
            act(1, node + s)

    for step in range(1, nodes):
        scale_copy(node, step).start()
    for p in range(parts + 1):

        @pl.when(has_up)
        def _(p=p):
            z_copy(0, node, p).start()

        @pl.when(has_down)
        def _(p=p):
            z_copy(1, node, p).start()

    def accumulate_first(slot):
        def one_tile(j, carry):
            place = pl.ds(pl.multiple_of(j * tile, tile), tile)
            x = jnp.concatenate([raw[slot, p, place, :] for p in range(parts)], axis=1)
            x_high, x_pair = paired(x)
            column_scale = scales[slot, pl.ds(j, 1), :]
            for t in range(row_tiles):
                place = t * col_tiles + slot * row_tiles + j
                a = tiles[t, slot_of[place]] * (column_scale * live[place])
                first[t * tile : (t + 1) * tile, :] += product(a, x_high, x_pair)
            return carry

        lax.fori_loop(0, row_tiles, one_tile, 0)

    for block in range(rows // LANES):
        lanes = slice(block * LANES, (block + 1) * LANES)
        scale[lanes, :] = jnp.broadcast_to(row_scale[:, lanes], (LANES, LANES)).T
    for t in range(row_tiles):

        def find(c, carry, t=t):
            found, hits = jnp.int32(0), jnp.int32(0)
            for k in range(slots):
                hit = jnp.logical_and(tile_cols[0, t, k] == c, k < tile_count[0, t])
                found += k * hit.astype(jnp.int32)
                hits += hit.astype(jnp.int32)
            slot_of[t * col_tiles + c] = found
            live[t * col_tiles + c] = hits.astype(jnp.float32)
            return carry

        lax.fori_loop(0, col_tiles, find, 0)

    both_sides(1, take_z)
    first[...] = jnp.zeros_like(first)
    tiles_copy.wait()
    accumulate_first(node)

    def first_step(s, carry):
        both_sides(s + 1, take_z)
        both_sides(s, lambda way, slot: take_xy(slot))

        def use(way, slot):
            scale_copy(slot, 1).wait_recv()
            accumulate_first(slot)

        both_sides(s, use)
        return carry

    lax.fori_loop(1, nodes, first_step, 0)

    def line_copy(stage, way, slot):
        neighbour = node + 1 if way == 0 else node - 1
        ref = field.at[stage, slot]
        return remote(
            ref, ref, line_send.at[stage, way, slot], line_recv.at[stage, slot], node=neighbour
        )

    def send_up(stage, slot):
        @pl.when(has_up)
        def _():
            line_copy(stage, 0, slot).start()

    def send_down(stage, slot):
        @pl.when(has_down)
        def _():
            line_copy(stage, 1, slot).start()

    def accumulate(stage, slot):
        def one_tile(j, carry):
            x = field[stage, slot, pl.ds(pl.multiple_of(j * tile, tile), tile), :]
            x_high, x_pair = paired(x)
            for t in range(row_tiles):
                place = t * col_tiles + slot * row_tiles + j
                a = tiles[t, slot_of[place]] * live[place]
                total[t * tile : (t + 1) * tile, :] += product(a, x_high, x_pair)
            return carry

        lax.fori_loop(0, row_tiles, one_tile, 0)

    def hop(stage):
        total[...] = jnp.zeros_like(total)
        accumulate(stage, node)

        def step(s, carry):
            @pl.when(node - s >= 0)
            def _():
                line_copy(stage, 0, node - s).wait_recv()
                send_up(stage, node - s)

            @pl.when(node + s < nodes)
            def _():
                line_copy(stage, 1, node + s).wait_recv()
                send_down(stage, node + s)

            both_sides(s, lambda way, slot: accumulate(stage, slot))
            return carry

        lax.fori_loop(1, nodes, step, 0)

    def project(side, chunk, target):
        start = pl.multiple_of((side * chunks + chunk) * LANES, LANES)
        w_high, w_pair = paired(weight[:, pl.ds(start, LANES)])

        def some_rows(j, carry):
            place = pl.ds(pl.multiple_of(j * tile, tile), tile)
            target[place, :] = product(first[place, :], w_high, w_pair)
            return carry

        lax.fori_loop(0, row_tiles, some_rows, 0)

    def pair_copy(chunk):
        return remote(
            partial_out.at[chunk],
            partial_in.at[chunk],
            pair_send.at[chunk],
            pair_recv.at[chunk],
            feat=1 - feat,
        )

    def give(chunk):
        project(1 - feat, chunk, partial_out.at[chunk])
        pair_copy(chunk).start()

    give(0)
    for chunk in range(chunks):
        project(feat, chunk, field.at[chunk, node])
        if chunk + 1 < chunks:
            give(chunk + 1)
        pair_copy(chunk).wait_recv()
        field[chunk, node] = scale[...] * (
            scale[...] * (field[chunk, node] + partial_in[chunk])
        )
        send_up(chunk, node)
        send_down(chunk, node)

    def out_copy(chunk, step):
        peer = lax.rem(rel + step, rels)
        return remote(
            result.at[chunk, pl.ds(pl.multiple_of(peer * group, 8), group), :],
            out.at[rel, :, pl.ds(chunk * LANES, LANES)],
            out_send.at[chunk, step],
            out_recv.at[chunk, step],
            rel=peer,
        )

    def in_copy(chunk, step):
        peer = lax.rem(rel + rels - step, rels)
        return remote(
            result.at[chunk, pl.ds(0, group), :],
            out.at[peer, :, pl.ds(chunk * LANES, LANES)],
            out_send.at[chunk, step],
            out_recv.at[chunk, step],
            rel=peer,
        )

    for chunk in range(chunks):
        hop(chunk)
        columns = slice(chunk * LANES, (chunk + 1) * LANES)
        result[chunk] = scale[...] * total[...] + bias[:, columns]
        for step in range(1, rels):
            out_copy(chunk, step).start()
        own = pl.ds(pl.multiple_of(rel * group, 8), group)
        out[rel, :, columns] = result[chunk, own, :]

    for step in range(1, nodes):
        scale_copy(node, step).wait_send()

    def drain(slot, carry):
        def waits(way):
            for p in range(parts + 1):
                z_copy(way, slot, p).wait_send()
            for stage in range(chunks):
                line_copy(stage, way, slot).wait_send()

        @pl.when(jnp.logical_and(has_up, slot <= node))
        def _():
            waits(0)

        @pl.when(jnp.logical_and(has_down, slot >= node))
        def _():
            waits(1)

        @pl.when(slot != node)
        def _():
            for p in range(parts + 1):
                x_out(slot, p).wait_send()
                y_out(slot, p).wait_send()

        return carry

    lax.fori_loop(0, nodes, drain, 0)
    for chunk in range(chunks):
        pair_copy(chunk).wait_send()
        for step in range(1, rels):
            out_copy(chunk, step).wait_send()
            in_copy(chunk, step).wait_recv()


def on_device(
    nodes, rels, features, tile_values, tile_cols, tile_count, degree, proj_weight, proj_bias
):
    rows, depth = features.shape
    _, row_tiles, slots, tile, _ = tile_values.shape
    width = proj_bias.shape[1]
    chunks = width // LANES
    col_tiles = nodes * row_tiles
    parts = depth // LANES
    vmem = pl.BlockSpec(memory_space=pltpu.VMEM)
    smem = pl.BlockSpec(memory_space=pltpu.SMEM)
    dma = pltpu.SemaphoreType.DMA
    return pl.pallas_call(
        functools.partial(kernel, (nodes, rels, chunks)),
        out_shape=jax.ShapeDtypeStruct((rels, rows // rels, width), jnp.float32),
        in_specs=[smem, smem, vmem, vmem, vmem] + [pl.BlockSpec(memory_space=pl.ANY)] * 2,
        out_specs=vmem,
        scratch_shapes=[
            pltpu.SMEM((row_tiles * col_tiles,), jnp.int32),
            pltpu.SMEM((row_tiles * col_tiles,), jnp.float32),
            pltpu.VMEM((rows, LANES), jnp.float32),
            pltpu.VMEM((row_tiles, slots, tile, tile), jnp.float32),
            pltpu.VMEM((nodes, parts, rows, LANES), jnp.float32),
            pltpu.VMEM((nodes, SUBLANES, tile), jnp.float32),
            pltpu.VMEM((rows, depth), jnp.float32),
            pltpu.VMEM((chunks, nodes, rows, LANES), jnp.float32),
            pltpu.VMEM((rows, LANES), jnp.float32),
            pltpu.VMEM((chunks, rows, LANES), jnp.float32),
            pltpu.VMEM((chunks, rows, LANES), jnp.float32),
            pltpu.VMEM((chunks, rows, LANES), jnp.float32),
            dma((parts + 1,)),
            dma((nodes,)),
            dma((nodes,)),
            dma((2, nodes, parts + 1)),
            dma((nodes, parts + 1)),
            dma((nodes, parts + 1)),
            dma((nodes, parts + 1)),
            dma((nodes, parts + 1)),
            dma((nodes, parts + 1)),
            dma((chunks,)),
            dma((chunks,)),
            dma((chunks, 2, nodes)),
            dma((chunks, nodes)),
            dma((chunks, rels)),
            dma((chunks, rels)),
        ],
        compiler_params=pltpu.CompilerParams(
            collective_id=0, has_side_effects=True, vmem_limit_bytes=56 << 20
        ),
    )(
        tile_cols,
        tile_count,
        degree,
        proj_weight[0],
        proj_bias,
        features,
        tile_values[0],
    )


def solution(mesh):
    return jax.shard_map(
        functools.partial(on_device, mesh.shape["node"], mesh.shape["rel"]),
        mesh=mesh,
        in_specs=(
            P("node", "feat"),
            P("rel", "node", None, None, None),
            P("rel", "node", None),
            P("rel", "node"),
            P("rel", "node"),
            P("rel", "feat", None),
            P("rel", "feat"),
        ),
        out_specs=P(None, ("node", "rel"), "feat"),
        check_vma=False,
    )
```

```python
import functools

import jax
import jax.numpy as jnp
from jax import lax
from jax.experimental import pallas as pl
from jax.experimental.pallas import tpu as pltpu
from jax.sharding import PartitionSpec as P

MESH = pl.DeviceIdType.MESH
LANES = 128
SUBLANES = 8


def split(x):
    high = x.astype(jnp.bfloat16)
    return high, (x - high.astype(jnp.float32)).astype(jnp.bfloat16)


def paired(x):
    high, low = split(x)
    return high, jnp.concatenate([high, low], axis=1)


def product(a, x_high, x_pair):
    a_high, a_low = split(a)
    width = x_high.shape[1]
    both = jnp.dot(a_high, x_pair, preferred_element_type=jnp.float32)
    rest = jnp.dot(a_low, x_high, preferred_element_type=jnp.float32)
    return both[:, :width] + both[:, width:] + rest


def kernel(
    sizes,
    tile_cols,
    tile_count,
    degree,
    weight,
    bias,
    features_hbm,
    tiles_hbm,
    out,
    slot_of,
    live,
    scale,
    tiles,
    raw,
    scales,
    first,
    field,
    total,
    result,
    partial_out,
    partial_in,
    load_sem,
    scale_send,
    scale_recv,
    z_send,
    z_recv,
    x_send,
    x_recv,
    y_send,
    y_recv,
    pair_send,
    pair_recv,
    line_send,
    line_recv,
    out_send,
    out_recv,
):
    nodes, rels, chunks = sizes
    parts, rows = raw.shape[1:3]
    slots = tiles.shape[1]
    tile = tiles.shape[2]
    row_tiles = tiles.shape[0]
    col_tiles = nodes * row_tiles
    group = rows // rels
    rel, node, feat = (lax.axis_index(name) for name in ("rel", "node", "feat"))
    has_up, has_down = node < nodes - 1, node > 0
    x_rel, y_rel, far_rel = rel + 1 - 2 * lax.rem(rel, 2), lax.rem(rel + 2, rels), rels - 1 - rel

    barrier = pltpu.get_barrier_semaphore()
    pl.semaphore_signal(barrier, inc=1, device_id={"feat": 1 - feat}, device_id_type=MESH)
    for step in range(1, rels):
        peer = lax.rem(rel + step, rels)
        pl.semaphore_signal(barrier, inc=1, device_id={"rel": peer}, device_id_type=MESH)
    for step in range(1, nodes):
        peer = lax.rem(node + step, nodes)
        pl.semaphore_signal(barrier, inc=1, device_id={"node": peer}, device_id_type=MESH)
    features_copies = [
        pltpu.make_async_copy(
            features_hbm.at[:, pl.ds(p * LANES, LANES)], raw.at[node, p], load_sem.at[p]
        )
        for p in range(parts)
    ]
    for copy in features_copies:
        copy.start()
    tiles_copy = pltpu.make_async_copy(tiles_hbm, tiles, load_sem.at[parts])
    tiles_copy.start()
    row_scale = lax.rsqrt(degree[...].astype(jnp.float32))
    scales[node] = jnp.zeros(scales.shape[1:], jnp.float32)
    for t in range(row_tiles):
        scales[node, t : t + 1, :] = row_scale[:, t * tile : (t + 1) * tile]
    for copy in features_copies:
        copy.wait()
    pl.semaphore_wait(barrier, rels + nodes - 1)

    def remote(src, dst, send_sem, recv_sem, **device):
        return pltpu.make_async_remote_copy(
            src_ref=src,
            dst_ref=dst,
            send_sem=send_sem,
            recv_sem=recv_sem,
            device_id=device,
            device_id_type=MESH,
        )

    def scale_copy(slot, step):
        peer = lax.rem(node + step, nodes)
        return remote(
            scales.at[slot], scales.at[slot], scale_send.at[step], scale_recv.at[slot], node=peer
        )

    def piece(slot, quarter, part):
        place = pl.ds(pl.multiple_of(quarter * group, 8), group)
        return raw.at[slot, part, place, :]

    def z_copy(way, slot, p):
        ref = piece(slot, rel, p) if p < parts else piece(slot, far_rel, 0)
        neighbour = node + 1 if way == 0 else node - 1
        return remote(ref, ref, z_send.at[way, slot, p], z_recv.at[slot, p], node=neighbour)

    def x_copy(slot, p, near, far):
        ref = piece(slot, near, p) if p < parts else piece(slot, far, 1)
        return remote(ref, ref, x_send.at[slot, p], x_recv.at[slot, p], rel=x_rel)

    def y_copy(slot, p, near, far):
        ref = piece(slot, near, p) if p < parts else piece(slot, far, 2)
        return remote(ref, ref, y_send.at[slot, p], y_recv.at[slot, p], rel=y_rel)

    def x_out(slot, p):
        return x_copy(slot, p, rel, y_rel)

    def x_in(slot, p):
        return x_copy(slot, p, x_rel, far_rel)

    def y_out(slot, p):
        return y_copy(slot, p, rel, x_rel)

    def y_in(slot, p):
        return y_copy(slot, p, y_rel, far_rel)

    def take_z(way, slot, p):
        z_copy(way, slot, p).wait_recv()

        @pl.when(has_up if way == 0 else has_down)
        def _():
            z_copy(way, slot, p).start()

        if p < parts:
            x_out(slot, p).start()
            y_out(slot, p).start()

    def take_nearest(way, slot):
        for p in range(parts + 1):
            take_z(way, slot, p)

    def advance(way, slot):
        beyond = slot - 1 if way == 0 else slot + 1
        for p in range(parts + 1):

            @pl.when(slot > 0 if way == 0 else slot < nodes - 1)
            def _(p=p):
                take_z(way, beyond, p)

            x_in(slot, p).wait_recv()
            if p == 2:
                y_out(slot, parts).start()
            y_in(slot, p).wait_recv()
            if p == 1:
                x_out(slot, parts).start()

    def both_sides(s, act):
        @pl.when(node - s >= 0)
        def _():
            act(0, node - s)

        @pl.when(node + s < nodes)
        def _():
            act(1, node + s)

    for step in range(1, nodes):
        scale_copy(node, step).start()
    for p in range(parts + 1):

        @pl.when(has_up)
        def _(p=p):
            z_copy(0, node, p).start()

        @pl.when(has_down)
        def _(p=p):
            z_copy(1, node, p).start()

    def accumulate_first(slot):
        def one_tile(j, carry):
            place = pl.ds(pl.multiple_of(j * tile, tile), tile)
            x = jnp.concatenate([raw[slot, p, place, :] for p in range(parts)], axis=1)
            x_high, x_pair = paired(x)
            column_scale = scales[slot, pl.ds(j, 1), :]
            for t in range(row_tiles):
                place = t * col_tiles + slot * row_tiles + j
                a = tiles[t, slot_of[place]] * (column_scale * live[place])
                first[t * tile : (t + 1) * tile, :] += product(a, x_high, x_pair)
            return carry

        lax.fori_loop(0, row_tiles, one_tile, 0)

    for block in range(rows // LANES):
        lanes = slice(block * LANES, (block + 1) * LANES)
        scale[lanes, :] = jnp.broadcast_to(row_scale[:, lanes], (LANES, LANES)).T
    for t in range(row_tiles):

        def find(c, carry, t=t):
            found, hits = jnp.int32(0), jnp.int32(0)
            for k in range(slots):
                hit = jnp.logical_and(tile_cols[0, t, k] == c, k < tile_count[0, t])
                found += k * hit.astype(jnp.int32)
                hits += hit.astype(jnp.int32)
            slot_of[t * col_tiles + c] = found
            live[t * col_tiles + c] = hits.astype(jnp.float32)
            return carry

        lax.fori_loop(0, col_tiles, find, 0)

    both_sides(1, take_nearest)
    first[...] = jnp.zeros_like(first)
    tiles_copy.wait()
    accumulate_first(node)

    def first_step(s, carry):
        both_sides(s, advance)

        def use(way, slot):
            scale_copy(slot, 1).wait_recv()
            accumulate_first(slot)

        both_sides(s, use)
        return carry

    lax.fori_loop(1, nodes, first_step, 0)

    def line_copy(stage, way, slot):
        neighbour = node + 1 if way == 0 else node - 1
        ref = field.at[stage, slot]
        return remote(
            ref, ref, line_send.at[stage, way, slot], line_recv.at[stage, slot], node=neighbour
        )

    def send_up(stage, slot):
        @pl.when(has_up)
        def _():
            line_copy(stage, 0, slot).start()

    def send_down(stage, slot):
        @pl.when(has_down)
        def _():
            line_copy(stage, 1, slot).start()

    def accumulate(stage, slot):
        def one_tile(j, carry):
            x = field[stage, slot, pl.ds(pl.multiple_of(j * tile, tile), tile), :]
            x_high, x_pair = paired(x)
            for t in range(row_tiles):
                place = t * col_tiles + slot * row_tiles + j
                a = tiles[t, slot_of[place]] * live[place]
                total[t * tile : (t + 1) * tile, :] += product(a, x_high, x_pair)
            return carry

        lax.fori_loop(0, row_tiles, one_tile, 0)

    def hop(stage):
        total[...] = jnp.zeros_like(total)
        accumulate(stage, node)

        def step(s, carry):
            @pl.when(node - s >= 0)
            def _():
                line_copy(stage, 0, node - s).wait_recv()
                send_up(stage, node - s)

            @pl.when(node + s < nodes)
            def _():
                line_copy(stage, 1, node + s).wait_recv()
                send_down(stage, node + s)

            both_sides(s, lambda way, slot: accumulate(stage, slot))
            return carry

        lax.fori_loop(1, nodes, step, 0)

    def project(side, chunk, target):
        start = pl.multiple_of((side * chunks + chunk) * LANES, LANES)
        w_high, w_pair = paired(weight[:, pl.ds(start, LANES)])

        def some_rows(j, carry):
            place = pl.ds(pl.multiple_of(j * tile, tile), tile)
            target[place, :] = product(first[place, :], w_high, w_pair)
            return carry

        lax.fori_loop(0, row_tiles, some_rows, 0)

    def pair_copy(chunk):
        return remote(
            partial_out.at[chunk],
            partial_in.at[chunk],
            pair_send.at[chunk],
            pair_recv.at[chunk],
            feat=1 - feat,
        )

    def give(chunk):
        project(1 - feat, chunk, partial_out.at[chunk])
        pair_copy(chunk).start()

    give(0)
    for chunk in range(chunks):
        project(feat, chunk, field.at[chunk, node])
        if chunk + 1 < chunks:
            give(chunk + 1)
        pair_copy(chunk).wait_recv()
        field[chunk, node] = scale[...] * (
            scale[...] * (field[chunk, node] + partial_in[chunk])
        )
        send_up(chunk, node)
        send_down(chunk, node)

    def out_copy(chunk, step):
        peer = lax.rem(rel + step, rels)
        return remote(
            result.at[chunk, pl.ds(pl.multiple_of(peer * group, 8), group), :],
            out.at[rel, :, pl.ds(chunk * LANES, LANES)],
            out_send.at[chunk, step],
            out_recv.at[chunk, step],
            rel=peer,
        )

    def in_copy(chunk, step):
        peer = lax.rem(rel + rels - step, rels)
        return remote(
            result.at[chunk, pl.ds(0, group), :],
            out.at[peer, :, pl.ds(chunk * LANES, LANES)],
            out_send.at[chunk, step],
            out_recv.at[chunk, step],
            rel=peer,
        )

    for chunk in range(chunks):
        hop(chunk)
        columns = slice(chunk * LANES, (chunk + 1) * LANES)
        result[chunk] = scale[...] * total[...] + bias[:, columns]
        for step in range(1, rels):
            out_copy(chunk, step).start()
        own = pl.ds(pl.multiple_of(rel * group, 8), group)
        out[rel, :, columns] = result[chunk, own, :]

    for step in range(1, nodes):
        scale_copy(node, step).wait_send()

    def drain(slot, carry):
        def waits(way):
            for p in range(parts + 1):
                z_copy(way, slot, p).wait_send()
            for stage in range(chunks):
                line_copy(stage, way, slot).wait_send()

        @pl.when(jnp.logical_and(has_up, slot <= node))
        def _():
            waits(0)

        @pl.when(jnp.logical_and(has_down, slot >= node))
        def _():
            waits(1)

        @pl.when(slot != node)
        def _():
            for p in range(parts + 1):
                x_out(slot, p).wait_send()
                y_out(slot, p).wait_send()

        return carry

    lax.fori_loop(0, nodes, drain, 0)
    for chunk in range(chunks):
        pair_copy(chunk).wait_send()
        for step in range(1, rels):
            out_copy(chunk, step).wait_send()
            in_copy(chunk, step).wait_recv()


def on_device(
    nodes, rels, features, tile_values, tile_cols, tile_count, degree, proj_weight, proj_bias
):
    rows, depth = features.shape
    _, row_tiles, slots, tile, _ = tile_values.shape
    width = proj_bias.shape[1]
    chunks = width // LANES
    col_tiles = nodes * row_tiles
    parts = depth // LANES
    vmem = pl.BlockSpec(memory_space=pltpu.VMEM)
    smem = pl.BlockSpec(memory_space=pltpu.SMEM)
    dma = pltpu.SemaphoreType.DMA
    return pl.pallas_call(
        functools.partial(kernel, (nodes, rels, chunks)),
        out_shape=jax.ShapeDtypeStruct((rels, rows // rels, width), jnp.float32),
        in_specs=[smem, smem, vmem, vmem, vmem] + [pl.BlockSpec(memory_space=pl.ANY)] * 2,
        out_specs=vmem,
        scratch_shapes=[
            pltpu.SMEM((row_tiles * col_tiles,), jnp.int32),
            pltpu.SMEM((row_tiles * col_tiles,), jnp.float32),
            pltpu.VMEM((rows, LANES), jnp.float32),
            pltpu.VMEM((row_tiles, slots, tile, tile), jnp.float32),
            pltpu.VMEM((nodes, parts, rows, LANES), jnp.float32),
            pltpu.VMEM((nodes, SUBLANES, tile), jnp.float32),
            pltpu.VMEM((rows, depth), jnp.float32),
            pltpu.VMEM((chunks, nodes, rows, LANES), jnp.float32),
            pltpu.VMEM((rows, LANES), jnp.float32),
            pltpu.VMEM((chunks, rows, LANES), jnp.float32),
            pltpu.VMEM((chunks, rows, LANES), jnp.float32),
            pltpu.VMEM((chunks, rows, LANES), jnp.float32),
            dma((parts + 1,)),
            dma((nodes,)),
            dma((nodes,)),
            dma((2, nodes, parts + 1)),
            dma((nodes, parts + 1)),
            dma((nodes, parts + 1)),
            dma((nodes, parts + 1)),
            dma((nodes, parts + 1)),
            dma((nodes, parts + 1)),
            dma((chunks,)),
            dma((chunks,)),
            dma((chunks, 2, nodes)),
            dma((chunks, nodes)),
            dma((chunks, rels)),
            dma((chunks, rels)),
        ],
        compiler_params=pltpu.CompilerParams(
            collective_id=0, has_side_effects=True, vmem_limit_bytes=56 << 20
        ),
    )(
        tile_cols,
        tile_count,
        degree,
        proj_weight[0],
        proj_bias,
        features,
        tile_values[0],
    )


def solution(mesh):
    return jax.shard_map(
        functools.partial(on_device, mesh.shape["node"], mesh.shape["rel"]),
        mesh=mesh,
        in_specs=(
            P("node", "feat"),
            P("rel", "node", None, None, None),
            P("rel", "node", None),
            P("rel", "node"),
            P("rel", "node"),
            P("rel", "feat", None),
            P("rel", "feat"),
        ),
        out_specs=P(None, ("node", "rel"), "feat"),
        check_vma=False,
    )
```

```python
import functools

import jax
import jax.numpy as jnp
from jax import lax
from jax.experimental import pallas as pl
from jax.experimental.pallas import tpu as pltpu
from jax.sharding import PartitionSpec as P

MESH = pl.DeviceIdType.MESH
LANES = 128
SUBLANES = 8


def split(x):
    high = x.astype(jnp.bfloat16)
    return high, (x - high.astype(jnp.float32)).astype(jnp.bfloat16)


def paired(x):
    high, low = split(x)
    return high, jnp.concatenate([high, low], axis=1)


def product(a, x_high, x_pair):
    a_high, a_low = split(a)
    width = x_high.shape[1]
    both = jnp.dot(a_high, x_pair, preferred_element_type=jnp.float32)
    rest = jnp.dot(a_low, x_high, preferred_element_type=jnp.float32)
    return both[:, :width] + both[:, width:] + rest


def kernel(
    sizes,
    tile_cols,
    tile_count,
    degree,
    weight,
    bias,
    features_hbm,
    tiles_hbm,
    out,
    slot_of,
    live,
    scale,
    tiles,
    raw,
    scales,
    first,
    field,
    total,
    result,
    partial_out,
    partial_in,
    load_sem,
    scale_send,
    scale_recv,
    z_send,
    z_recv,
    x_send,
    x_recv,
    y_send,
    y_recv,
    pair_send,
    pair_recv,
    line_send,
    line_recv,
    out_send,
    out_recv,
):
    nodes, rels, chunks = sizes
    parts, rows = raw.shape[1:3]
    slots = tiles.shape[1]
    tile = tiles.shape[2]
    row_tiles = tiles.shape[0]
    col_tiles = nodes * row_tiles
    group = rows // rels
    rel, node, feat = (lax.axis_index(name) for name in ("rel", "node", "feat"))
    has_up, has_down = node < nodes - 1, node > 0
    x_rel, y_rel, far_rel = rel + 1 - 2 * lax.rem(rel, 2), lax.rem(rel + 2, rels), rels - 1 - rel

    barrier = pltpu.get_barrier_semaphore()
    pl.semaphore_signal(barrier, inc=1, device_id={"feat": 1 - feat}, device_id_type=MESH)
    for step in range(1, rels):
        peer = lax.rem(rel + step, rels)
        pl.semaphore_signal(barrier, inc=1, device_id={"rel": peer}, device_id_type=MESH)
    for step in range(1, nodes):
        peer = lax.rem(node + step, nodes)
        pl.semaphore_signal(barrier, inc=1, device_id={"node": peer}, device_id_type=MESH)
    features_copies = [
        pltpu.make_async_copy(
            features_hbm.at[:, pl.ds(p * LANES, LANES)], raw.at[node, p], load_sem.at[p]
        )
        for p in range(parts)
    ]
    for copy in features_copies:
        copy.start()
    tiles_copy = pltpu.make_async_copy(tiles_hbm, tiles, load_sem.at[parts])
    tiles_copy.start()
    row_scale = lax.rsqrt(degree[...].astype(jnp.float32))
    scales[node] = jnp.zeros(scales.shape[1:], jnp.float32)
    for t in range(row_tiles):
        scales[node, t : t + 1, :] = row_scale[:, t * tile : (t + 1) * tile]
    for copy in features_copies:
        copy.wait()
    pl.semaphore_wait(barrier, rels + nodes - 1)

    def remote(src, dst, send_sem, recv_sem, **device):
        return pltpu.make_async_remote_copy(
            src_ref=src,
            dst_ref=dst,
            send_sem=send_sem,
            recv_sem=recv_sem,
            device_id=device,
            device_id_type=MESH,
        )

    def scale_copy(slot, step):
        peer = lax.rem(node + step, nodes)
        return remote(
            scales.at[slot], scales.at[slot], scale_send.at[step], scale_recv.at[slot], node=peer
        )

    def piece(slot, quarter, part):
        place = pl.ds(pl.multiple_of(quarter * group, 8), group)
        return raw.at[slot, part, place, :]

    def z_copy(way, slot, p):
        ref = piece(slot, rel, p) if p < parts else piece(slot, far_rel, 0)
        neighbour = node + 1 if way == 0 else node - 1
        return remote(ref, ref, z_send.at[way, slot, p], z_recv.at[slot, p], node=neighbour)

    def x_copy(slot, p, near, far):
        ref = piece(slot, near, p) if p < parts else piece(slot, far, 1)
        return remote(ref, ref, x_send.at[slot, p], x_recv.at[slot, p], rel=x_rel)

    def y_copy(slot, p, near, far):
        ref = piece(slot, near, p) if p < parts else piece(slot, far, 2)
        return remote(ref, ref, y_send.at[slot, p], y_recv.at[slot, p], rel=y_rel)

    def x_out(slot, p):
        return x_copy(slot, p, rel, y_rel)

    def x_in(slot, p):
        return x_copy(slot, p, x_rel, far_rel)

    def y_out(slot, p):
        return y_copy(slot, p, rel, x_rel)

    def y_in(slot, p):
        return y_copy(slot, p, y_rel, far_rel)

    def take_z(way, slot):
        onward = has_up if way == 0 else has_down
        for p in range(parts + 1):
            z_copy(way, slot, p).wait_recv()

            @pl.when(onward)
            def _(p=p):
                z_copy(way, slot, p).start()

            if p < parts:
                x_out(slot, p).start()
                y_out(slot, p).start()

    def take_xy(slot):
        for p in range(parts):
            x_in(slot, p).wait_recv()
            if p == 2:
                y_out(slot, parts).start()
            y_in(slot, p).wait_recv()
            if p == 1:
                x_out(slot, parts).start()
        x_in(slot, parts).wait_recv()
        y_in(slot, parts).wait_recv()

    def both_sides(s, act):
        @pl.when(node - s >= 0)
        def _():
            act(0, node - s)

        @pl.when(node + s < nodes)
        def _():
            act(1, node + s)

    for step in range(1, nodes):
        scale_copy(node, step).start()
    for p in range(parts + 1):

        @pl.when(has_up)
        def _(p=p):
            z_copy(0, node, p).start()

        @pl.when(has_down)
        def _(p=p):
            z_copy(1, node, p).start()

    def accumulate_first(slot):
        def one_tile(j, carry):
            place = pl.ds(pl.multiple_of(j * tile, tile), tile)
            x = jnp.concatenate([raw[slot, p, place, :] for p in range(parts)], axis=1)
            x_high, x_pair = paired(x)
            column_scale = scales[slot, pl.ds(j, 1), :]
            for t in range(row_tiles):
                place = t * col_tiles + slot * row_tiles + j
                a = tiles[t, slot_of[place]] * (column_scale * live[place])
                first[t * tile : (t + 1) * tile, :] += product(a, x_high, x_pair)
            return carry

        lax.fori_loop(0, row_tiles, one_tile, 0)

    both_sides(1, take_z)
    for block in range(rows // LANES):
        lanes = slice(block * LANES, (block + 1) * LANES)
        scale[lanes, :] = jnp.broadcast_to(row_scale[:, lanes], (LANES, LANES)).T
    for t in range(row_tiles):

        def find(c, carry, t=t):
            found, hits = jnp.int32(0), jnp.int32(0)
            for k in range(slots):
                hit = jnp.logical_and(tile_cols[0, t, k] == c, k < tile_count[0, t])
                found += k * hit.astype(jnp.int32)
                hits += hit.astype(jnp.int32)
            slot_of[t * col_tiles + c] = found
            live[t * col_tiles + c] = hits.astype(jnp.float32)
            return carry

        lax.fori_loop(0, col_tiles, find, 0)

    first[...] = jnp.zeros_like(first)
    tiles_copy.wait()
    accumulate_first(node)

    def first_step(s, carry):
        both_sides(s + 1, take_z)
        both_sides(s, lambda way, slot: take_xy(slot))

        def use(way, slot):
            scale_copy(slot, 1).wait_recv()
            accumulate_first(slot)

        both_sides(s, use)
        return carry

    lax.fori_loop(1, nodes, first_step, 0)

    def line_copy(stage, way, slot):
        neighbour = node + 1 if way == 0 else node - 1
        ref = field.at[stage, slot]
        return remote(
            ref, ref, line_send.at[stage, way, slot], line_recv.at[stage, slot], node=neighbour
        )

    def send_up(stage, slot):
        @pl.when(has_up)
        def _():
            line_copy(stage, 0, slot).start()

    def send_down(stage, slot):
        @pl.when(has_down)
        def _():
            line_copy(stage, 1, slot).start()

    def accumulate(stage, slot):
        def one_tile(j, carry):
            x = field[stage, slot, pl.ds(pl.multiple_of(j * tile, tile), tile), :]
            x_high, x_pair = paired(x)
            for t in range(row_tiles):
                place = t * col_tiles + slot * row_tiles + j
                a = tiles[t, slot_of[place]] * live[place]
                total[t * tile : (t + 1) * tile, :] += product(a, x_high, x_pair)
            return carry

        lax.fori_loop(0, row_tiles, one_tile, 0)

    def hop(stage):
        total[...] = jnp.zeros_like(total)
        accumulate(stage, node)

        def step(s, carry):
            @pl.when(node - s >= 0)
            def _():
                line_copy(stage, 0, node - s).wait_recv()
                send_up(stage, node - s)

            @pl.when(node + s < nodes)
            def _():
                line_copy(stage, 1, node + s).wait_recv()
                send_down(stage, node + s)

            both_sides(s, lambda way, slot: accumulate(stage, slot))
            return carry

        lax.fori_loop(1, nodes, step, 0)

    def project(side, chunk, target):
        start = pl.multiple_of((side * chunks + chunk) * LANES, LANES)
        w_high, w_pair = paired(weight[:, pl.ds(start, LANES)])

        def some_rows(j, carry):
            place = pl.ds(pl.multiple_of(j * tile, tile), tile)
            target[place, :] = product(first[place, :], w_high, w_pair)
            return carry

        lax.fori_loop(0, row_tiles, some_rows, 0)

    def pair_copy(chunk):
        return remote(
            partial_out.at[chunk],
            partial_in.at[chunk],
            pair_send.at[chunk],
            pair_recv.at[chunk],
            feat=1 - feat,
        )

    def give(chunk):
        project(1 - feat, chunk, partial_out.at[chunk])
        pair_copy(chunk).start()

    give(0)
    for chunk in range(chunks):
        project(feat, chunk, field.at[chunk, node])
        if chunk + 1 < chunks:
            give(chunk + 1)
        pair_copy(chunk).wait_recv()
        field[chunk, node] = scale[...] * (
            scale[...] * (field[chunk, node] + partial_in[chunk])
        )
        send_up(chunk, node)
        send_down(chunk, node)

    def out_copy(chunk, step):
        peer = lax.rem(rel + step, rels)
        return remote(
            result.at[chunk, pl.ds(pl.multiple_of(peer * group, 8), group), :],
            out.at[rel, :, pl.ds(chunk * LANES, LANES)],
            out_send.at[chunk, step],
            out_recv.at[chunk, step],
            rel=peer,
        )

    def in_copy(chunk, step):
        peer = lax.rem(rel + rels - step, rels)
        return remote(
            result.at[chunk, pl.ds(0, group), :],
            out.at[peer, :, pl.ds(chunk * LANES, LANES)],
            out_send.at[chunk, step],
            out_recv.at[chunk, step],
            rel=peer,
        )

    for chunk in range(chunks):
        hop(chunk)
        columns = slice(chunk * LANES, (chunk + 1) * LANES)
        result[chunk] = scale[...] * total[...] + bias[:, columns]
        for step in range(1, rels):
            out_copy(chunk, step).start()
        own = pl.ds(pl.multiple_of(rel * group, 8), group)
        out[rel, :, columns] = result[chunk, own, :]

    for step in range(1, nodes):
        scale_copy(node, step).wait_send()

    def drain(slot, carry):
        def waits(way):
            for p in range(parts + 1):
                z_copy(way, slot, p).wait_send()
            for stage in range(chunks):
                line_copy(stage, way, slot).wait_send()

        @pl.when(jnp.logical_and(has_up, slot <= node))
        def _():
            waits(0)

        @pl.when(jnp.logical_and(has_down, slot >= node))
        def _():
            waits(1)

        @pl.when(slot != node)
        def _():
            for p in range(parts + 1):
                x_out(slot, p).wait_send()
                y_out(slot, p).wait_send()

        return carry

    lax.fori_loop(0, nodes, drain, 0)
    for chunk in range(chunks):
        pair_copy(chunk).wait_send()
        for step in range(1, rels):
            out_copy(chunk, step).wait_send()
            in_copy(chunk, step).wait_recv()


def on_device(
    nodes, rels, features, tile_values, tile_cols, tile_count, degree, proj_weight, proj_bias
):
    rows, depth = features.shape
    _, row_tiles, slots, tile, _ = tile_values.shape
    width = proj_bias.shape[1]
    chunks = width // LANES
    col_tiles = nodes * row_tiles
    parts = depth // LANES
    vmem = pl.BlockSpec(memory_space=pltpu.VMEM)
    smem = pl.BlockSpec(memory_space=pltpu.SMEM)
    dma = pltpu.SemaphoreType.DMA
    return pl.pallas_call(
        functools.partial(kernel, (nodes, rels, chunks)),
        out_shape=jax.ShapeDtypeStruct((rels, rows // rels, width), jnp.float32),
        in_specs=[smem, smem, vmem, vmem, vmem] + [pl.BlockSpec(memory_space=pl.ANY)] * 2,
        out_specs=vmem,
        scratch_shapes=[
            pltpu.SMEM((row_tiles * col_tiles,), jnp.int32),
            pltpu.SMEM((row_tiles * col_tiles,), jnp.float32),
            pltpu.VMEM((rows, LANES), jnp.float32),
            pltpu.VMEM((row_tiles, slots, tile, tile), jnp.float32),
            pltpu.VMEM((nodes, parts, rows, LANES), jnp.float32),
            pltpu.VMEM((nodes, SUBLANES, tile), jnp.float32),
            pltpu.VMEM((rows, depth), jnp.float32),
            pltpu.VMEM((chunks, nodes, rows, LANES), jnp.float32),
            pltpu.VMEM((rows, LANES), jnp.float32),
            pltpu.VMEM((chunks, rows, LANES), jnp.float32),
            pltpu.VMEM((chunks, rows, LANES), jnp.float32),
            pltpu.VMEM((chunks, rows, LANES), jnp.float32),
            dma((parts + 1,)),
            dma((nodes,)),
            dma((nodes,)),
            dma((2, nodes, parts + 1)),
            dma((nodes, parts + 1)),
            dma((nodes, parts + 1)),
            dma((nodes, parts + 1)),
            dma((nodes, parts + 1)),
            dma((nodes, parts + 1)),
            dma((chunks,)),
            dma((chunks,)),
            dma((chunks, 2, nodes)),
            dma((chunks, nodes)),
            dma((chunks, rels)),
            dma((chunks, rels)),
        ],
        compiler_params=pltpu.CompilerParams(
            collective_id=0, has_side_effects=True, vmem_limit_bytes=56 << 20
        ),
    )(
        tile_cols,
        tile_count,
        degree,
        proj_weight[0],
        proj_bias,
        features,
        tile_values[0],
    )


def solution(mesh):
    return jax.shard_map(
        functools.partial(on_device, mesh.shape["node"], mesh.shape["rel"]),
        mesh=mesh,
        in_specs=(
            P("node", "feat"),
            P("rel", "node", None, None, None),
            P("rel", "node", None),
            P("rel", "node"),
            P("rel", "node"),
            P("rel", "feat", None),
            P("rel", "feat"),
        ),
        out_specs=P(None, ("node", "rel"), "feat"),
        check_vma=False,
    )
```
